1024 devices in a mesh: seq: 128 (over y, z_lo, core), head: 8 (over z_hi, x).
Axes of the slice: x: 4, y: 4, z: 32 (z_hi: 2, z_lo: 16; z = z_hi * 16 + z_lo), core: 2. Of those that a mesh axis runs over, the one named last changes fastest.
Arguments:
- queries: bfloat16 [16384, 64, 576], P('seq', 'head'), may hold values from -64 to 64
- latent: bfloat16 [16384, 576], P('seq'), may hold values from -8 to 8
- grad_out: bfloat16 [16384, 64, 512], P('seq', 'head'), may hold values from -6 to 6
- lookback: int32 [16384], P('seq'), may hold values from 0 to 256
Outputs:
- grad_queries: bfloat16 [16384, 64, 576], P('seq', 'head')
- grad_latent: bfloat16 [16384, 576], P('seq')
The draws below stay inside these ranges and needn't reach their ends.
All inputs are finite; a program needn't handle non-finite values.
Results may differ from the reference program's by a relative error of at most 0.0049.
Values may be sent and summed in bfloat16 or wider, within the bound.
No kernel may reach another device: no remote copies, remote signals or barrier semaphores. Data moves between devices by JAX's collectives and lax.ppermute only.
A program may use at most 32 MiB of HBM per device.

```python
import jax
import jax.numpy as jnp
from jax import lax

LATENT = 512
ROPE = 64
NOPE = 128
TOK_DEV = 128
KEY_DIM = 576
HEADS = 64
TOKENS = 16384
N_SEQ = 128


def paired_draw(key):
    base = jax.random.fold_in(key, 11)
    latent_key, query_key = jax.random.split(base, 2)
    latent = jnp.clip(jax.random.normal(latent_key, (TOKENS, KEY_DIM), jnp.float32), -6.0, 6.0)
    queries = jnp.clip(jax.random.normal(query_key, (TOKENS, HEADS, KEY_DIM), jnp.float32), -6.0, 6.0)
    return (latent, queries)


def draw_queries(key, part):
    return paired_draw(key)[1].astype(jnp.bfloat16)


def draw_latent(key, part):
    return paired_draw(key)[0].astype(jnp.bfloat16)


def touch_ends(array, key, least, largest):
    spot = [jax.random.randint(jax.random.fold_in(key, axis), (), 0, length) for axis, length in enumerate(array.shape)]
    main_axis = array.shape.index(max(array.shape))
    next_to = spot[:main_axis] + [(spot[main_axis] + 1) % array.shape[main_axis]] + spot[main_axis + 1:]
    return array.at[tuple(spot)].set(least).at[tuple(next_to)].set(largest)


def steps_of(key, dims, shards, smallest, high):
    loudness, own = 1.0, jax.random.fold_in(key, 6)
    for position, parts in shards:
        heights = jnp.exp(jax.random.uniform(jax.random.fold_in(own, position), (parts,), jnp.float32, smallest / len(shards), high / len(shards)))
        loudness = loudness * jnp.repeat(heights, dims[position] // parts).reshape([-1 if axis == position else 1 for axis in range(len(dims))])
    return loudness


def gaussian(own_key, extent, width, limit, cuts=(), kind=jnp.bfloat16):
    entries = width * jax.random.normal(own_key, extent, jnp.float32)
    if cuts:
        entries = entries * steps_of(own_key, extent, cuts, -0.22, 0.18)
    return jnp.clip(entries, -limit, limit).astype(kind)


def setup_inputs(seed: int = 0) -> dict:
    keys = jax.random.split(jax.random.key(seed), 5)
    queries = draw_queries(jax.random.fold_in(keys[4], 71), 0)
    latent = draw_latent(jax.random.fold_in(keys[4], 71), 0)
    grad_out = gaussian(keys[2], (TOKENS, HEADS, LATENT), 1.0, 6.0, ((0, 128), (1, 8)))
    lookback = touch_ends(jax.random.randint(keys[3], (TOKENS,), 0, 2 * TOK_DEV + 1), jax.random.fold_in(keys[3], 1), 0, 2 * TOK_DEV).astype(jnp.int32)
    return {"queries": queries, "latent": latent, "grad_out": grad_out, "lookback": lookback}


def reference(queries, latent, grad_out, lookback):
    score_scale = (NOPE + ROPE) ** -0.5
    padding = jnp.zeros((2 * TOK_DEV, KEY_DIM), jnp.bfloat16)
    key_source = jnp.concatenate([padding, latent], axis=0)
    initial = jnp.zeros((TOKENS + 2 * TOK_DEV, KEY_DIM), jnp.float32)

    def advance(carried, block_id):
        first_row = (block_id * TOK_DEV).astype(jnp.int32)
        query_rows = lax.dynamic_slice_in_dim(queries, first_row, TOK_DEV, 0).reshape(TOK_DEV * HEADS, KEY_DIM)
        grad_rows = lax.dynamic_slice_in_dim(grad_out, first_row, TOK_DEV, 0).reshape(TOK_DEV * HEADS, LATENT)
        reach = lax.dynamic_slice_in_dim(lookback, first_row, TOK_DEV, 0)
        key_rows = lax.dynamic_slice_in_dim(key_source, first_row, 3 * TOK_DEV, 0)
        query_pos = first_row + jnp.arange(TOK_DEV, dtype=jnp.int32)
        key_pos = first_row - 2 * TOK_DEV + jnp.arange(3 * TOK_DEV, dtype=jnp.int32)
        allowed = (key_pos[None, :] >= 0) & (key_pos[None, :] <= query_pos[:, None]) & (key_pos[None, :] >= query_pos[:, None] - reach[:, None])
        allowed = jnp.broadcast_to(allowed[:, None, :], (TOK_DEV, HEADS, 3 * TOK_DEV)).reshape(TOK_DEV * HEADS, 3 * TOK_DEV)
        scores = jnp.dot(query_rows, key_rows.T, preferred_element_type=jnp.float32) * score_scale
        masked = jnp.where(allowed, scores, -jnp.inf)
        highest = jnp.max(masked, axis=-1, keepdims=True)
        weights = jnp.exp(masked - highest)
        weights = weights / jnp.sum(weights, axis=-1, keepdims=True)
        grad_weights = jnp.dot(grad_rows, key_rows[:, :LATENT].T, preferred_element_type=jnp.float32)
        row_dot = jnp.sum(weights * grad_weights, axis=-1, keepdims=True)
        grad_scores = (weights * (grad_weights - row_dot) * score_scale).astype(jnp.bfloat16)
        weights_half = weights.astype(jnp.bfloat16)
        grad_query = jnp.dot(grad_scores, key_rows, preferred_element_type=jnp.float32).astype(jnp.bfloat16)
        grad_keys = jnp.dot(grad_scores.T, query_rows, preferred_element_type=jnp.float32)
        grad_values = jnp.dot(weights_half.T, grad_rows, preferred_element_type=jnp.float32)
        combined = grad_keys + jnp.pad(grad_values, ((0, 0), (0, ROPE)))
        window = lax.dynamic_slice_in_dim(carried, first_row, 3 * TOK_DEV, 0)
        carried = lax.dynamic_update_slice_in_dim(carried, window + combined, first_row, 0)
        return carried, grad_query

    carried, grad_blocks = lax.scan(advance, initial, jnp.arange(N_SEQ, dtype=jnp.int32))
    grad_queries = grad_blocks.reshape(TOKENS, HEADS, KEY_DIM)
    grad_latent = carried[2 * TOK_DEV:].astype(jnp.bfloat16)
    return grad_queries, grad_latent
```

```python
import jax
import jax.numpy as jnp
from jax import lax
from jax.experimental import pallas as pl
from jax.experimental.pallas import tpu as pltpu
from jax.sharding import PartitionSpec as P

ROPE = 64
NOPE = 128
BF = jnp.bfloat16
F32 = jnp.float32
Z_LO, CORES, Z_HI, X = 16, 2, 2, 4
BOTH = ("seq", "head")
VMEM = pl.BlockSpec(memory_space=pltpu.VMEM)


def shifted_pairs(seq_size, steps):
    run = Z_LO * CORES
    heads = Z_HI * X
    pairs = []
    for source in range(seq_size):
        target = source + steps
        if not 0 <= target < seq_size:
            continue
        for z_hi in range(Z_HI):
            for x in range(X):
                other = z_hi if source // run == target // run else 1 - z_hi
                pairs.append((source * heads + z_hi * X + x, target * heads + other * X + x))
    return pairs


def dot_rows(a, b):
    return lax.dot_general(a, b, (((1,), (1,)), ((), ())), preferred_element_type=F32)


def grad_kernel(q_ref, do_ref, far_ref, near_ref, own_ref, low_ref, dl_ref, ds_ref, keys_ref, p_ref):
    heads, _, tok = q_ref.shape
    value = do_ref.shape[1]
    span = 3 * tok
    scale = (NOPE + ROPE) ** (-0.5)
    for block, ref in enumerate((far_ref, near_ref, own_ref)):
        keys_ref[block * tok : (block + 1) * tok, :] = ref[...].T
    row = lax.broadcasted_iota(jnp.int32, (span, tok), 0) - 2 * tok
    col = lax.broadcasted_iota(jnp.int32, (span, tok), 1)
    allowed = (row <= col) & (row >= low_ref[...])
    for pair in range(0, heads, 2):
        q2 = jnp.concatenate([q_ref[pair], q_ref[pair + 1]], axis=1)
        do2 = jnp.concatenate([do_ref[pair], do_ref[pair + 1]], axis=1)
        scores = jnp.dot(keys_ref[...], q2, preferred_element_type=F32)
        grad_weights = jnp.dot(keys_ref[:, :value], do2, preferred_element_type=F32)
        for half in range(2):
            lanes = slice(half * tok, (half + 1) * tok)
            masked = jnp.where(allowed, scores[:, lanes], -jnp.inf)
            highest = jnp.max(masked, axis=0, keepdims=True)
            weights = jnp.exp((masked - highest) * scale)
            weights = weights * (1.0 / jnp.sum(weights, axis=0, keepdims=True))
            row_dot = jnp.sum(weights * grad_weights[:, lanes], axis=0, keepdims=True)
            here = slice((pair + half) * tok, (pair + half + 1) * tok)
            p_ref[:, here] = weights.astype(BF)
            ds_ref[:, here] = (weights * (grad_weights[:, lanes] - row_dot) * scale).astype(BF)
    q_all = jnp.concatenate([q_ref[h] for h in range(heads)], axis=1)
    do_all = jnp.concatenate([do_ref[h] for h in range(heads)], axis=1)
    upper = dot_rows(q_all[:value], ds_ref[...]) + dot_rows(do_all, p_ref[...])
    lower = dot_rows(q_all[value:], ds_ref[...])
    total = jnp.concatenate([upper, lower], axis=0).astype(BF)
    part = dl_ref.shape[1] // 3
    for piece in range(dl_ref.shape[0]):
        for back in range(3):
            dl_ref[piece, back * part : (back + 1) * part, :] = total[
                piece * part : (piece + 1) * part, (2 - back) * tok : (3 - back) * tok
            ]


def query_kernel(far_ref, near_ref, own_ref, ds_ref, dq_ref):
    heads, _, tok = dq_ref.shape
    keys = jnp.concatenate([far_ref[...], near_ref[...], own_ref[...]], axis=1)
    for pair in range(0, heads, 2):
        out = jnp.dot(keys, ds_ref[:, pair * tok : (pair + 2) * tok], preferred_element_type=F32)
        dq_ref[pair] = out[:, :tok].astype(BF)
        dq_ref[pair + 1] = out[:, tok:].astype(BF)


def on_device(queries, latent, grad_out, lookback):
    tok, heads, width = queries.shape
    value = grad_out.shape[2]
    rows = heads * tok
    seq_size = lax.axis_size("seq")
    own = latent.T
    near = lax.ppermute(own, BOTH, shifted_pairs(seq_size, 1))
    far = lax.ppermute(own, BOTH, shifted_pairs(seq_size, 2))
    first_row = (lax.axis_index("seq") * tok).astype(jnp.int32)
    low = jnp.maximum(jnp.arange(tok, dtype=jnp.int32) - lookback, -first_row)[None, :]
    part = width // X
    partial_sums, grad_scores = pl.pallas_call(
        grad_kernel,
        out_shape=(
            jax.ShapeDtypeStruct((X, 3 * part, tok), BF),
            jax.ShapeDtypeStruct((3 * tok, rows), BF),
        ),
        in_specs=[VMEM] * 6,
        out_specs=(VMEM, VMEM),
        scratch_shapes=[pltpu.VMEM((3 * tok, width), BF), pltpu.VMEM((3 * tok, rows), BF)],
        compiler_params=pltpu.CompilerParams(vmem_limit_bytes=40 * 2**20),
        cost_estimate=pl.CostEstimate(
            flops=2 * rows * 3 * tok * (2 * width + 2 * value),
            bytes_accessed=2 * rows * (width + value + 3 * tok),
            transcendentals=rows * 3 * tok,
        ),
        name="grads",
    )(queries.transpose(1, 2, 0), grad_out.transpose(1, 2, 0), far, near, own, low)

    along_x = [[z_hi * X + x for x in range(X)] for z_hi in range(Z_HI)]
    pieces = lax.all_to_all(partial_sums, "head", 0, 0, axis_index_groups=along_x)
    sums = jnp.sum(pieces.astype(F32), axis=0)
    to_near = lax.ppermute(sums[part : 2 * part].astype(BF), BOTH, shifted_pairs(seq_size, -1))
    to_far = lax.ppermute(sums[2 * part :].astype(BF), BOTH, shifted_pairs(seq_size, -2))
    half_sum = (sums[:part] + to_near.astype(F32) + to_far.astype(F32)).astype(BF)
    across = [(h, (h + X) % (Z_HI * X)) for h in range(Z_HI * X)]
    other_half = lax.ppermute(half_sum, "head", across)
    grad_queries = pl.pallas_call(
        query_kernel,
        out_shape=jax.ShapeDtypeStruct((heads, width, tok), BF),
        in_specs=[VMEM] * 4,
        out_specs=VMEM,
        compiler_params=pltpu.CompilerParams(vmem_limit_bytes=40 * 2**20),
        cost_estimate=pl.CostEstimate(
            flops=2 * rows * 3 * tok * width, bytes_accessed=2 * rows * (width + 3 * tok), transcendentals=0
        ),
        name="dquery",
    )(far, near, own, grad_scores)
    quarter = (half_sum.astype(F32) + other_half.astype(F32)).astype(BF)
    grad_latent = lax.all_to_all(
        jnp.broadcast_to(quarter[None], (X, part, tok)), "head", 0, 0, axis_index_groups=along_x
    )
    return (grad_queries.transpose(2, 0, 1), grad_latent.reshape(width, tok).T)


def solution(mesh):
    return jax.shard_map(
        on_device,
        mesh=mesh,
        in_specs=(P("seq", "head", None), P("seq", None), P("seq", "head", None), P("seq")),
        out_specs=(P("seq", "head", None), P("seq", None)),
        check_vma=False,
    )
```

```python
import jax
import jax.numpy as jnp
from jax import lax
from jax.experimental import pallas as pl
from jax.experimental.pallas import tpu as pltpu
from jax.sharding import PartitionSpec as P

ROPE = 64
NOPE = 128
BF = jnp.bfloat16
F32 = jnp.float32
LOG2_E = 1.4426950408889634
Z_LO, CORES, Z_HI, X = 16, 2, 2, 4
BOTH = ("seq", "head")
VMEM = pl.BlockSpec(memory_space=pltpu.VMEM)


def shifted_pairs(seq_size, steps):
    run = Z_LO * CORES
    heads = Z_HI * X
    pairs = []
    for source in range(seq_size):
        target = source + steps
        if not 0 <= target < seq_size:
            continue
        for z_hi in range(Z_HI):
            for x in range(X):
                other = z_hi if source // run == target // run else 1 - z_hi
                pairs.append((source * heads + z_hi * X + x, target * heads + other * X + x))
    return pairs


def dot_rows(a, b):
    return lax.dot_general(a, b, (((1,), (1,)), ((), ())), preferred_element_type=F32)


def score_kernel(q_ref, do_ref, near_ref, own_ref, s_ref, g_ref, keys_ref):
    heads, _, tok = q_ref.shape
    value = do_ref.shape[1]
    keys_ref[:tok, :] = near_ref[...].T
    keys_ref[tok:, :] = own_ref[...].T
    for pair in range(0, heads, 2):
        here = slice(pair * tok, (pair + 2) * tok)
        q2 = jnp.concatenate([q_ref[pair], q_ref[pair + 1]], axis=1)
        do2 = jnp.concatenate([do_ref[pair], do_ref[pair + 1]], axis=1)
        s_ref[:, here] = jnp.dot(keys_ref[...], q2, preferred_element_type=F32)
        g_ref[:, here] = jnp.dot(keys_ref[:, :value], do2, preferred_element_type=F32)


def grad_kernel(q_ref, do_ref, far_ref, s_ref, g_ref, low_ref, dl_ref, ds_ref, keys_ref, p_ref, bias_ref):
    heads, _, tok = q_ref.shape
    value = do_ref.shape[1]
    span = 3 * tok
    scale = (NOPE + ROPE) ** (-0.5)
    keys_ref[...] = far_ref[...].T
    row = lax.broadcasted_iota(jnp.int32, (span, tok), 0) - 2 * tok
    col = lax.broadcasted_iota(jnp.int32, (span, tok), 1)
    allowed = (row <= col) & (row >= low_ref[...])
    bias_ref[...] = jnp.where(allowed, 0.0, -jnp.inf).astype(F32)
    for pair in range(0, heads, 2):
        q2 = jnp.concatenate([q_ref[pair], q_ref[pair + 1]], axis=1)
        do2 = jnp.concatenate([do_ref[pair], do_ref[pair + 1]], axis=1)
        far_scores = jnp.dot(keys_ref[...], q2, preferred_element_type=F32)
        far_weights = jnp.dot(keys_ref[:, :value], do2, preferred_element_type=F32)
        for half in range(2):
            lanes = slice(half * tok, (half + 1) * tok)
            here = slice((pair + half) * tok, (pair + half + 1) * tok)
            scores = jnp.concatenate([far_scores[:, lanes], s_ref[:, here]], axis=0) + bias_ref[...]
            grad_weights = jnp.concatenate([far_weights[:, lanes], g_ref[:, here]], axis=0)
            highest = jnp.max(scores, axis=0, keepdims=True)
            raised = jnp.exp2((scores - highest) * (scale * LOG2_E))
            inverse = 1.0 / jnp.sum(raised, axis=0, keepdims=True)
            row_dot = jnp.sum(raised * grad_weights, axis=0, keepdims=True) * inverse
            weights = raised * inverse
            p_ref[:, here] = weights.astype(BF)
            ds_ref[:, here] = (weights * ((grad_weights - row_dot) * scale)).astype(BF)
    q_all = jnp.concatenate([q_ref[h] for h in range(heads)], axis=1)
    do_all = jnp.concatenate([do_ref[h] for h in range(heads)], axis=1)
    upper = dot_rows(q_all[:value], ds_ref[...]) + dot_rows(do_all, p_ref[...])
    lower = dot_rows(q_all[value:], ds_ref[...])
    total = jnp.concatenate([upper, lower], axis=0).astype(BF)
    part = dl_ref.shape[1] // 3
    for piece in range(dl_ref.shape[0]):
        for back in range(3):
            dl_ref[piece, back * part : (back + 1) * part, :] = total[
                piece * part : (piece + 1) * part, (2 - back) * tok : (3 - back) * tok
            ]


def finish_kernel(mine_ref, other_ref, out_ref):
    total = (mine_ref[...].astype(F32) + other_ref[...].astype(F32)).astype(BF)
    for piece in range(out_ref.shape[0]):
        out_ref[piece] = total


def query_kernel(far_ref, near_ref, own_ref, ds_ref, dq_ref):
    heads, _, tok = dq_ref.shape
    keys = jnp.concatenate([far_ref[...], near_ref[...], own_ref[...]], axis=1)
    for pair in range(0, heads, 2):
        out = jnp.dot(keys, ds_ref[:, pair * tok : (pair + 2) * tok], preferred_element_type=F32)
        dq_ref[pair] = out[:, :tok].astype(BF)
        dq_ref[pair + 1] = out[:, tok:].astype(BF)


def on_device(queries, latent, grad_out, lookback):
    tok, heads, width = queries.shape
    value = grad_out.shape[2]
    rows = heads * tok
    seq_size = lax.axis_size("seq")
    own = latent.T
    near = lax.ppermute(own, BOTH, shifted_pairs(seq_size, 1))
    far = lax.ppermute(own, BOTH, shifted_pairs(seq_size, 2))
    first_row = (lax.axis_index("seq") * tok).astype(jnp.int32)
    low = jnp.maximum(jnp.arange(tok, dtype=jnp.int32) - lookback, -first_row)[None, :]
    part = width // X
    turned_queries = queries.transpose(1, 2, 0)
    turned_grads = grad_out.transpose(1, 2, 0)
    params = pltpu.CompilerParams(vmem_limit_bytes=32 * 2**20)
    scores, grad_weights = pl.pallas_call(
        score_kernel,
        out_shape=(jax.ShapeDtypeStruct((2 * tok, rows), F32),) * 2,
        in_specs=[VMEM] * 4,
        out_specs=(VMEM, VMEM),
        scratch_shapes=[pltpu.VMEM((2 * tok, width), BF)],
        compiler_params=params,
        cost_estimate=pl.CostEstimate(
            flops=2 * rows * 2 * tok * (width + value),
            bytes_accessed=2 * rows * (width + value + 8 * tok),
            transcendentals=0,
        ),
        name="scores",
    )(turned_queries, turned_grads, near, own)
    partial_sums, grad_scores = pl.pallas_call(
        grad_kernel,
        out_shape=(
            jax.ShapeDtypeStruct((X, 3 * part, tok), BF),
            jax.ShapeDtypeStruct((3 * tok, rows), BF),
        ),
        in_specs=[VMEM] * 6,
        out_specs=(VMEM, VMEM),
        scratch_shapes=[
            pltpu.VMEM((tok, width), BF),
            pltpu.VMEM((3 * tok, rows), BF),
            pltpu.VMEM((3 * tok, tok), F32),
        ],
        compiler_params=params,
        cost_estimate=pl.CostEstimate(
            flops=2 * rows * tok * 4 * (width + value),
            bytes_accessed=2 * rows * (width + value + 11 * tok),
            transcendentals=rows * 3 * tok,
        ),
        name="grads",
    )(turned_queries, turned_grads, far, scores, grad_weights, low)

    along_x = [[z_hi * X + x for x in range(X)] for z_hi in range(Z_HI)]
    pieces = lax.all_to_all(partial_sums, "head", 0, 0, axis_index_groups=along_x)
    sums = jnp.sum(pieces.astype(F32), axis=0)
    to_near = lax.ppermute(sums[part : 2 * part].astype(BF), BOTH, shifted_pairs(seq_size, -1))
    to_far = lax.ppermute(sums[2 * part :].astype(BF), BOTH, shifted_pairs(seq_size, -2))
    half_sum = (sums[:part] + to_near.astype(F32) + to_far.astype(F32)).astype(BF)
    across = [(h, (h + X) % (Z_HI * X)) for h in range(Z_HI * X)]
    other_half = lax.ppermute(half_sum, "head", across)
    grad_queries = pl.pallas_call(
        query_kernel,
        out_shape=jax.ShapeDtypeStruct((heads, width, tok), BF),
        in_specs=[VMEM] * 4,
        out_specs=VMEM,
        compiler_params=params,
        cost_estimate=pl.CostEstimate(
            flops=2 * rows * 3 * tok * width, bytes_accessed=2 * rows * (width + 3 * tok), transcendentals=0
        ),
        name="dquery",
    )(far, near, own, grad_scores)
    other_half, grad_queries = lax.optimization_barrier((other_half, grad_queries))
    copies = pl.pallas_call(
        finish_kernel,
        out_shape=jax.ShapeDtypeStruct((X, part, tok), BF),
        in_specs=[VMEM] * 2,
        out_specs=VMEM,
        compiler_params=params,
        name="finish",
    )(half_sum, other_half)
    grad_latent = lax.all_to_all(copies, "head", 0, 0, axis_index_groups=along_x)
    return (grad_queries.transpose(2, 0, 1), grad_latent.reshape(width, tok).T)


def solution(mesh):
    return jax.shard_map(
        on_device,
        mesh=mesh,
        in_specs=(P("seq", "head", None), P("seq", None), P("seq", "head", None), P("seq")),
        out_specs=(P("seq", "head", None), P("seq", None)),
        check_vma=False,
    )
```

```python
import jax
import jax.numpy as jnp
from jax import lax
from jax.experimental import pallas as pl
from jax.experimental.pallas import tpu as pltpu
from jax.sharding import PartitionSpec as P

ROPE = 64
NOPE = 128
BF = jnp.bfloat16
F32 = jnp.float32
LOG2_E = 1.4426950408889634
Z_LO, CORES, Z_HI, X = 16, 2, 2, 4
BOTH = ("seq", "head")
VMEM = pl.BlockSpec(memory_space=pltpu.VMEM)


def shifted_pairs(seq_size, steps):
    run = Z_LO * CORES
    heads = Z_HI * X
    pairs = []
    for source in range(seq_size):
        target = source + steps
        if not 0 <= target < seq_size:
            continue
        for z_hi in range(Z_HI):
            for x in range(X):
                other = z_hi if source // run == target // run else 1 - z_hi
                pairs.append((source * heads + z_hi * X + x, target * heads + other * X + x))
    return pairs


def dot_rows(a, b):
    return lax.dot_general(a, b, (((1,), (1,)), ((), ())), preferred_element_type=F32)


def score_kernel(q_ref, do_ref, far_ref, own_ref, s_ref, g_ref, keys_ref):
    heads, _, tok = q_ref.shape
    value = do_ref.shape[1]
    keys_ref[:tok, :] = far_ref[...].T
    keys_ref[tok:, :] = own_ref[...].T
    for pair in range(0, heads, 2):
        here = slice(pair * tok, (pair + 2) * tok)
        q2 = jnp.concatenate([q_ref[pair], q_ref[pair + 1]], axis=1)
        do2 = jnp.concatenate([do_ref[pair], do_ref[pair + 1]], axis=1)
        s_ref[:, here] = jnp.dot(keys_ref[...], q2, preferred_element_type=F32)
        g_ref[:, here] = jnp.dot(keys_ref[:, :value], do2, preferred_element_type=F32)


def grad_kernel(
    q_ref, do_ref, near_ref, s_ref, g_ref, lookback_ref, far_out_ref, near_out_ref, own_out_ref, ds_ref, keys_ref, p_ref, bias_ref
):
    heads, _, tok = q_ref.shape
    value = do_ref.shape[1]
    span = 3 * tok
    scale = (NOPE + ROPE) ** (-0.5)
    keys_ref[...] = near_ref[...].T
    row = lax.broadcasted_iota(jnp.int32, (span, tok), 0) - 2 * tok
    col = lax.broadcasted_iota(jnp.int32, (span, tok), 1)
    first_row = lax.axis_index("seq") * tok
    allowed = (row <= col) & (row >= col - lookback_ref[...]) & (row >= -first_row)
    bias_ref[...] = jnp.where(allowed, 0.0, -jnp.inf).astype(F32)
    for pair in range(0, heads, 2):
        q2 = jnp.concatenate([q_ref[pair], q_ref[pair + 1]], axis=1)
        do2 = jnp.concatenate([do_ref[pair], do_ref[pair + 1]], axis=1)
        near_scores = jnp.dot(keys_ref[...], q2, preferred_element_type=F32)
        near_weights = jnp.dot(keys_ref[:, :value], do2, preferred_element_type=F32)
        for half in range(2):
            lanes = slice(half * tok, (half + 1) * tok)
            here = slice((pair + half) * tok, (pair + half + 1) * tok)
            scores = jnp.concatenate([s_ref[:tok, here], near_scores[:, lanes], s_ref[tok:, here]], axis=0)
            scores = scores + bias_ref[...]
            grad_weights = jnp.concatenate([g_ref[:tok, here], near_weights[:, lanes], g_ref[tok:, here]], axis=0)
            highest = jnp.max(scores, axis=0, keepdims=True)
            raised = jnp.exp2((scores - highest) * (scale * LOG2_E))
            inverse = 1.0 / jnp.sum(raised, axis=0, keepdims=True)
            row_dot = jnp.sum(raised * grad_weights, axis=0, keepdims=True) * inverse
            weights = raised * inverse
            p_ref[:, here] = weights.astype(BF)
            ds_ref[:, here] = (weights * ((grad_weights - row_dot) * scale)).astype(BF)
    q_all = jnp.concatenate([q_ref[h] for h in range(heads)], axis=1)
    do_all = jnp.concatenate([do_ref[h] for h in range(heads)], axis=1)
    upper = dot_rows(q_all[:value], ds_ref[...]) + dot_rows(do_all, p_ref[...])
    lower = dot_rows(q_all[value:], ds_ref[...])
    total = jnp.concatenate([upper, lower], axis=0)
    far_out_ref[...] = total[:, :tok].astype(BF)
    near_out_ref[...] = total[:, tok : 2 * tok].astype(BF)
    own_out_ref[...] = total[:, 2 * tok :]


def collect_kernel(own_ref, far_ref, near_ref, out_ref):
    half = out_ref.shape[1]
    for which in range(2):
        rows = slice(which * half, (which + 1) * half)
        total = (own_ref[rows] + near_ref[rows].astype(F32) + far_ref[rows].astype(F32)).astype(BF)
        for x in range(which, X, 2):
            out_ref[x] = total


def sum_kernel(pieces_ref, out_ref):
    total = pieces_ref[0].astype(F32)
    for x in range(1, X):
        total = total + pieces_ref[x].astype(F32)
    out_ref[...] = total.astype(BF)


def place_kernel(mine_ref, theirs_ref, out_ref):
    half = mine_ref.shape[0]
    odd = lax.axis_index("head") & 1
    out_ref[pl.ds(pl.multiple_of(odd * half, 16), half), :] = mine_ref[...]
    out_ref[pl.ds(pl.multiple_of((1 - odd) * half, 16), half), :] = theirs_ref[...]


def query_kernel(far_ref, near_ref, own_ref, ds_ref, dq_ref):
    heads, _, tok = dq_ref.shape
    keys = jnp.concatenate([far_ref[...], near_ref[...], own_ref[...]], axis=1)
    for pair in range(0, heads, 2):
        out = jnp.dot(keys, ds_ref[:, pair * tok : (pair + 2) * tok], preferred_element_type=F32)
        dq_ref[pair] = out[:, :tok].astype(BF)
        dq_ref[pair + 1] = out[:, tok:].astype(BF)


def on_device(queries, latent, grad_out, lookback):
    tok, heads, width = queries.shape
    value = grad_out.shape[2]
    rows = heads * tok
    seq_size = lax.axis_size("seq")
    own = latent.T
    far = lax.ppermute(own, BOTH, shifted_pairs(seq_size, 2))
    near = lax.ppermute(own, BOTH, shifted_pairs(seq_size, 1))
    half = width // 2
    turned_queries = queries.transpose(1, 2, 0)
    turned_grads = grad_out.transpose(1, 2, 0)
    params = pltpu.CompilerParams(vmem_limit_bytes=32 * 2**20)
    scores, grad_weights = pl.pallas_call(
        score_kernel,
        out_shape=(jax.ShapeDtypeStruct((2 * tok, rows), F32),) * 2,
        in_specs=[VMEM] * 4,
        out_specs=(VMEM, VMEM),
        scratch_shapes=[pltpu.VMEM((2 * tok, width), BF)],
        compiler_params=params,
        cost_estimate=pl.CostEstimate(
            flops=2 * rows * 2 * tok * (width + value),
            bytes_accessed=2 * rows * (width + value + 8 * tok),
            transcendentals=0,
        ),
        name="scores",
    )(turned_queries, turned_grads, far, own)
    part_far, part_near, part_own, grad_scores = pl.pallas_call(
        grad_kernel,
        out_shape=(
            jax.ShapeDtypeStruct((width, tok), BF),
            jax.ShapeDtypeStruct((width, tok), BF),
            jax.ShapeDtypeStruct((width, tok), F32),
            jax.ShapeDtypeStruct((3 * tok, rows), BF),
        ),
        in_specs=[VMEM] * 6,
        out_specs=(VMEM,) * 4,
        scratch_shapes=[
            pltpu.VMEM((tok, width), BF),
            pltpu.VMEM((3 * tok, rows), BF),
            pltpu.VMEM((3 * tok, tok), F32),
        ],
        compiler_params=params,
        cost_estimate=pl.CostEstimate(
            flops=2 * rows * tok * 4 * (width + value),
            bytes_accessed=2 * rows * (width + value + 11 * tok),
            transcendentals=rows * 3 * tok,
        ),
        name="grads",
    )(turned_queries, turned_grads, near, scores, grad_weights, lookback[None, :])

    to_far = lax.ppermute(part_far, BOTH, shifted_pairs(seq_size, -2))
    to_near = lax.ppermute(part_near, BOTH, shifted_pairs(seq_size, -1))
    halves = pl.pallas_call(
        collect_kernel,
        out_shape=jax.ShapeDtypeStruct((X, half, tok), BF),
        in_specs=[VMEM] * 3,
        out_specs=VMEM,
        compiler_params=params,
        name="collect",
    )(part_own, to_far, to_near)
    along_x = [[z_hi * X + x for x in range(X)] for z_hi in range(Z_HI)]
    pieces = lax.all_to_all(halves, "head", 0, 0, axis_index_groups=along_x)
    half_sum = pl.pallas_call(
        sum_kernel,
        out_shape=jax.ShapeDtypeStruct((half, tok), BF),
        in_specs=[VMEM],
        out_specs=VMEM,
        compiler_params=params,
        name="sum",
    )(pieces)
    across = [(h, (h + X) % (Z_HI * X)) for h in range(Z_HI * X)]
    other_half = lax.ppermute(half_sum, "head", across)
    grad_queries = pl.pallas_call(
        query_kernel,
        out_shape=jax.ShapeDtypeStruct((heads, width, tok), BF),
        in_specs=[VMEM] * 4,
        out_specs=VMEM,
        compiler_params=params,
        cost_estimate=pl.CostEstimate(
            flops=2 * rows * 3 * tok * width, bytes_accessed=2 * rows * (width + 3 * tok), transcendentals=0
        ),
        name="dquery",
    )(far, near, own, grad_scores)
    other_half, grad_queries = lax.optimization_barrier((other_half, grad_queries))
    mine = (half_sum.astype(F32) + other_half.astype(F32)).astype(BF)
    beside = [(h, h ^ 1) for h in range(Z_HI * X)]
    theirs = lax.ppermute(mine, "head", beside)
    grad_latent = pl.pallas_call(
        place_kernel,
        out_shape=jax.ShapeDtypeStruct((width, tok), BF),
        in_specs=[VMEM] * 2,
        out_specs=VMEM,
        compiler_params=params,
        name="place",
    )(mine, theirs)
    return (grad_queries.transpose(2, 0, 1), grad_latent.T)


def solution(mesh):
    return jax.shard_map(
        on_device,
        mesh=mesh,
        in_specs=(P("seq", "head", None), P("seq", None), P("seq", "head", None), P("seq")),
        out_specs=(P("seq", "head", None), P("seq", None)),
        check_vma=False,
    )
```

```python
import jax
import jax.numpy as jnp
from jax import lax
from jax.experimental import pallas as pl
from jax.experimental.pallas import tpu as pltpu
from jax.sharding import PartitionSpec as P

ROPE = 64
NOPE = 128
BF = jnp.bfloat16
F32 = jnp.float32
LOG2_E = 1.4426950408889634
Z_LO, CORES, Z_HI, X = 16, 2, 2, 4
BOTH = ("seq", "head")
VMEM = pl.BlockSpec(memory_space=pltpu.VMEM)


def shifted_pairs(seq_size, steps):
    run = Z_LO * CORES
    heads = Z_HI * X
    pairs = []
    for source in range(seq_size):
        target = source + steps
        if not 0 <= target < seq_size:
            continue
        for z_hi in range(Z_HI):
            for x in range(X):
                other = z_hi if source // run == target // run else 1 - z_hi
                pairs.append((source * heads + z_hi * X + x, target * heads + other * X + x))
    return pairs


def dot_rows(a, b):
    return lax.dot_general(a, b, (((1,), (1,)), ((), ())), preferred_element_type=F32)


def score_kernel(q_ref, do_ref, own_ref, s_ref, g_ref, keys_ref):
    heads, _, tok = q_ref.shape
    value = do_ref.shape[1]
    keys_ref[...] = own_ref[...].T
    for pair in range(0, heads, 2):
        here = slice(pair * tok, (pair + 2) * tok)
        q2 = jnp.concatenate([q_ref[pair], q_ref[pair + 1]], axis=1)
        do2 = jnp.concatenate([do_ref[pair], do_ref[pair + 1]], axis=1)
        s_ref[:, here] = jnp.dot(keys_ref[...], q2, preferred_element_type=F32)
        g_ref[:, here] = jnp.dot(keys_ref[:, :value], do2, preferred_element_type=F32)


def partials(q_ref, do_ref, ds, weights):
    heads = q_ref.shape[0]
    value = do_ref.shape[1]
    q_all = jnp.concatenate([q_ref[h] for h in range(heads)], axis=1)
    do_all = jnp.concatenate([do_ref[h] for h in range(heads)], axis=1)
    upper = dot_rows(q_all[:value], ds) + dot_rows(do_all, weights)
    return upper, dot_rows(q_all[value:], ds)


def grad_kernel(
    q_ref, do_ref, far_ref, near_ref, s_ref, g_ref, lookback_ref, far_out_ref, near_out_ref, p_ref, ds_ref, keys_ref, bias_ref
):
    heads, _, tok = q_ref.shape
    value = do_ref.shape[1]
    span = 3 * tok
    scale = (NOPE + ROPE) ** (-0.5)
    keys_ref[:tok, :] = far_ref[...].T
    keys_ref[tok:, :] = near_ref[...].T
    row = lax.broadcasted_iota(jnp.int32, (span, tok), 0) - 2 * tok
    col = lax.broadcasted_iota(jnp.int32, (span, tok), 1)
    first_row = lax.axis_index("seq") * tok
    allowed = (row <= col) & (row >= col - lookback_ref[...]) & (row >= -first_row)
    bias_ref[...] = jnp.where(allowed, 0.0, -jnp.inf).astype(F32)
    for pair in range(0, heads, 2):
        q2 = jnp.concatenate([q_ref[pair], q_ref[pair + 1]], axis=1)
        do2 = jnp.concatenate([do_ref[pair], do_ref[pair + 1]], axis=1)
        earlier_scores = jnp.dot(keys_ref[...], q2, preferred_element_type=F32)
        earlier_weights = jnp.dot(keys_ref[:, :value], do2, preferred_element_type=F32)
        for half in range(2):
            lanes = slice(half * tok, (half + 1) * tok)
            here = slice((pair + half) * tok, (pair + half + 1) * tok)
            scores = jnp.concatenate([earlier_scores[:, lanes], s_ref[:, here]], axis=0) + bias_ref[...]
            grad_weights = jnp.concatenate([earlier_weights[:, lanes], g_ref[:, here]], axis=0)
            highest = jnp.max(scores, axis=0, keepdims=True)
            raised = jnp.exp2((scores - highest) * (scale * LOG2_E))
            inverse = 1.0 / jnp.sum(raised, axis=0, keepdims=True)
            row_dot = jnp.sum(raised * grad_weights, axis=0, keepdims=True) * inverse
            weights = raised * inverse
            p_ref[:, here] = weights.astype(BF)
            ds_ref[:, here] = (weights * ((grad_weights - row_dot) * scale)).astype(BF)
    upper, lower = partials(q_ref, do_ref, ds_ref[: 2 * tok, :], p_ref[: 2 * tok, :])
    far_out_ref[:value] = upper[:, :tok].astype(BF)
    far_out_ref[value:] = lower[:, :tok].astype(BF)
    near_out_ref[:value] = upper[:, tok:].astype(BF)
    near_out_ref[value:] = lower[:, tok:].astype(BF)


def own_kernel(q_ref, do_ref, ds_ref, p_ref, out_ref):
    tok = q_ref.shape[2]
    value = do_ref.shape[1]
    upper, lower = partials(q_ref, do_ref, ds_ref[2 * tok :, :], p_ref[2 * tok :, :])
    out_ref[:value] = upper
    out_ref[value:] = lower


def collect_kernel(own_ref, far_ref, near_ref, out_ref):
    half = out_ref.shape[1]
    for which in range(2):
        rows = slice(which * half, (which + 1) * half)
        total = (own_ref[rows] + near_ref[rows].astype(F32) + far_ref[rows].astype(F32)).astype(BF)
        for x in range(which, X, 2):
            out_ref[x] = total


def sum_kernel(pieces_ref, out_ref):
    total = pieces_ref[0].astype(F32)
    for x in range(1, X):
        total = total + pieces_ref[x].astype(F32)
    out_ref[...] = total.astype(BF)


def place_kernel(mine_ref, theirs_ref, out_ref):
    half = mine_ref.shape[0]
    odd = lax.axis_index("head") & 1
    out_ref[pl.ds(pl.multiple_of(odd * half, 16), half), :] = mine_ref[...]
    out_ref[pl.ds(pl.multiple_of((1 - odd) * half, 16), half), :] = theirs_ref[...]


def query_kernel(far_ref, near_ref, own_ref, ds_ref, dq_ref):
    heads, _, tok = dq_ref.shape
    keys = jnp.concatenate([far_ref[...], near_ref[...], own_ref[...]], axis=1)
    for pair in range(0, heads, 2):
        out = jnp.dot(keys, ds_ref[:, pair * tok : (pair + 2) * tok], preferred_element_type=F32)
        dq_ref[pair] = out[:, :tok].astype(BF)
        dq_ref[pair + 1] = out[:, tok:].astype(BF)


def on_device(queries, latent, grad_out, lookback):
    tok, heads, width = queries.shape
    value = grad_out.shape[2]
    rows = heads * tok
    seq_size = lax.axis_size("seq")
    own = latent.T
    far = lax.ppermute(own, BOTH, shifted_pairs(seq_size, 2))
    near = lax.ppermute(own, BOTH, shifted_pairs(seq_size, 1))
    half = width // 2
    turned_queries = queries.transpose(1, 2, 0)
    turned_grads = grad_out.transpose(1, 2, 0)
    params = pltpu.CompilerParams(vmem_limit_bytes=32 * 2**20)
    scores, grad_weights = pl.pallas_call(
        score_kernel,
        out_shape=(jax.ShapeDtypeStruct((tok, rows), F32),) * 2,
        in_specs=[VMEM] * 3,
        out_specs=(VMEM, VMEM),
        scratch_shapes=[pltpu.VMEM((tok, width), BF)],
        compiler_params=params,
        cost_estimate=pl.CostEstimate(
            flops=2 * rows * tok * (width + value),
            bytes_accessed=2 * rows * (width + value + 4 * tok),
            transcendentals=0,
        ),
        name="scores",
    )(turned_queries, turned_grads, own)
    near, far, scores, grad_weights = lax.optimization_barrier((near, far, scores, grad_weights))
    part_far, part_near, weights_half, grad_scores = pl.pallas_call(
        grad_kernel,
        out_shape=(
            jax.ShapeDtypeStruct((width, tok), BF),
            jax.ShapeDtypeStruct((width, tok), BF),
            jax.ShapeDtypeStruct((3 * tok, rows), BF),
            jax.ShapeDtypeStruct((3 * tok, rows), BF),
        ),
        in_specs=[VMEM] * 7,
        out_specs=(VMEM,) * 4,
        scratch_shapes=[pltpu.VMEM((2 * tok, width), BF), pltpu.VMEM((3 * tok, tok), F32)],
        compiler_params=params,
        cost_estimate=pl.CostEstimate(
            flops=2 * rows * tok * 4 * (width + value),
            bytes_accessed=2 * rows * (width + value + 10 * tok),
            transcendentals=rows * 3 * tok,
        ),
        name="grads",
    )(turned_queries, turned_grads, far, near, scores, grad_weights, lookback[None, :])

    to_far = lax.ppermute(part_far, BOTH, shifted_pairs(seq_size, -2))
    to_near = lax.ppermute(part_near, BOTH, shifted_pairs(seq_size, -1))
    part_own = pl.pallas_call(
        own_kernel,
        out_shape=jax.ShapeDtypeStruct((width, tok), F32),
        in_specs=[VMEM] * 4,
        out_specs=VMEM,
        compiler_params=params,
        cost_estimate=pl.CostEstimate(
            flops=2 * rows * tok * (width + value),
            bytes_accessed=2 * rows * (width + value + 2 * tok),
            transcendentals=0,
        ),
        name="own",
    )(turned_queries, turned_grads, grad_scores, weights_half)
    halves = pl.pallas_call(
        collect_kernel,
        out_shape=jax.ShapeDtypeStruct((X, half, tok), BF),
        in_specs=[VMEM] * 3,
        out_specs=VMEM,
        compiler_params=params,
        name="collect",
    )(part_own, to_far, to_near)
    along_x = [[z_hi * X + x for x in range(X)] for z_hi in range(Z_HI)]
    pieces = lax.all_to_all(halves, "head", 0, 0, axis_index_groups=along_x)
    half_sum = pl.pallas_call(
        sum_kernel,
        out_shape=jax.ShapeDtypeStruct((half, tok), BF),
        in_specs=[VMEM],
        out_specs=VMEM,
        compiler_params=params,
        name="sum",
    )(pieces)
    across = [(h, (h + X) % (Z_HI * X)) for h in range(Z_HI * X)]
    other_half = lax.ppermute(half_sum, "head", across)
    grad_queries = pl.pallas_call(
        query_kernel,
        out_shape=jax.ShapeDtypeStruct((heads, width, tok), BF),
        in_specs=[VMEM] * 4,
        out_specs=VMEM,
        compiler_params=params,
        cost_estimate=pl.CostEstimate(
            flops=2 * rows * 3 * tok * width, bytes_accessed=2 * rows * (width + 3 * tok), transcendentals=0
        ),
        name="dquery",
    )(far, near, own, grad_scores)
    other_half, grad_queries = lax.optimization_barrier((other_half, grad_queries))
    mine = (half_sum.astype(F32) + other_half.astype(F32)).astype(BF)
    beside = [(h, h ^ 1) for h in range(Z_HI * X)]
    theirs = lax.ppermute(mine, "head", beside)
    grad_latent = pl.pallas_call(
        place_kernel,
        out_shape=jax.ShapeDtypeStruct((width, tok), BF),
        in_specs=[VMEM] * 2,
        out_specs=VMEM,
        compiler_params=params,
        name="place",
    )(mine, theirs)
    return (grad_queries.transpose(2, 0, 1), grad_latent.T)


def solution(mesh):
    return jax.shard_map(
        on_device,
        mesh=mesh,
        in_specs=(P("seq", "head", None), P("seq", None), P("seq", "head", None), P("seq")),
        out_specs=(P("seq", "head", None), P("seq", None)),
        check_vma=False,
    )
```

```python
import jax
import jax.numpy as jnp
from jax import lax
from jax.experimental import pallas as pl
from jax.experimental.pallas import tpu as pltpu
from jax.sharding import PartitionSpec as P

ROPE = 64
NOPE = 128
BF = jnp.bfloat16
F32 = jnp.float32
LOG2_E = 1.4426950408889634
Z_LO, CORES, Z_HI, X = 16, 2, 2, 4
BOTH = ("seq", "head")
VMEM = pl.BlockSpec(memory_space=pltpu.VMEM)


def shifted_pairs(seq_size, steps):
    run = Z_LO * CORES
    heads = Z_HI * X
    pairs = []
    for source in range(seq_size):
        target = source + steps
        if not 0 <= target < seq_size:
            continue
        for z_hi in range(Z_HI):
            for x in range(X):
                other = z_hi if source // run == target // run else 1 - z_hi
                pairs.append((source * heads + z_hi * X + x, target * heads + other * X + x))
    return pairs


def dot_rows(a, b):
    return lax.dot_general(a, b, (((1,), (1,)), ((), ())), preferred_element_type=F32)


def score_kernel(q_ref, do_ref, own_ref, s_ref, g_ref, keys_ref):
    heads, _, tok = q_ref.shape
    value = do_ref.shape[1]
    keys_ref[...] = own_ref[...].T
    for pair in range(0, heads, 2):
        here = slice(pair * tok, (pair + 2) * tok)
        q2 = jnp.concatenate([q_ref[pair], q_ref[pair + 1]], axis=1)
        do2 = jnp.concatenate([do_ref[pair], do_ref[pair + 1]], axis=1)
        s_ref[:, here] = jnp.dot(keys_ref[...], q2, preferred_element_type=F32)
        g_ref[:, here] = jnp.dot(keys_ref[:, :value], do2, preferred_element_type=F32)


def partials(q_ref, do_ref, ds, weights):
    heads = q_ref.shape[0]
    value = do_ref.shape[1]
    q_all = jnp.concatenate([q_ref[h] for h in range(heads)], axis=1)
    do_all = jnp.concatenate([do_ref[h] for h in range(heads)], axis=1)
    upper = dot_rows(q_all[:value], ds) + dot_rows(do_all, weights)
    return upper, dot_rows(q_all[value:], ds)


def grad_kernel(
    q_ref, do_ref, far_ref, near_ref, s_ref, g_ref, lookback_ref, far_out_ref, near_out_ref, p_ref, ds_ref, keys_ref, bias_ref
):
    heads, _, tok = q_ref.shape
    value = do_ref.shape[1]
    span = 3 * tok
    scale = (NOPE + ROPE) ** (-0.5)
    keys_ref[:tok, :] = far_ref[...].T
    keys_ref[tok:, :] = near_ref[...].T
    row = lax.broadcasted_iota(jnp.int32, (span, tok), 0) - 2 * tok
    col = lax.broadcasted_iota(jnp.int32, (span, tok), 1)
    first_row = lax.axis_index("seq") * tok
    allowed = (row <= col) & (row >= col - lookback_ref[...]) & (row >= -first_row)
    bias_ref[...] = jnp.where(allowed, 0.0, -jnp.inf).astype(F32)
    for pair in range(0, heads, 2):
        q2 = jnp.concatenate([q_ref[pair], q_ref[pair + 1]], axis=1)
        do2 = jnp.concatenate([do_ref[pair], do_ref[pair + 1]], axis=1)
        earlier_scores = jnp.dot(keys_ref[...], q2, preferred_element_type=F32)
        earlier_weights = jnp.dot(keys_ref[:, :value], do2, preferred_element_type=F32)
        for half in range(2):
            lanes = slice(half * tok, (half + 1) * tok)
            here = slice((pair + half) * tok, (pair + half + 1) * tok)
            scores = jnp.concatenate([earlier_scores[:, lanes], s_ref[:, here]], axis=0) + bias_ref[...]
            grad_weights = jnp.concatenate([earlier_weights[:, lanes], g_ref[:, here]], axis=0)
            highest = jnp.max(scores, axis=0, keepdims=True)
            raised = jnp.exp2((scores - highest) * (scale * LOG2_E))
            inverse = 1.0 / jnp.sum(raised, axis=0, keepdims=True)
            row_dot = jnp.sum(raised * grad_weights, axis=0, keepdims=True) * inverse
            weights = raised * inverse
            p_ref[:, here] = weights.astype(BF)
            ds_ref[:, here] = (weights * ((grad_weights - row_dot) * scale)).astype(BF)
    upper, lower = partials(q_ref, do_ref, ds_ref[: 2 * tok, :], p_ref[: 2 * tok, :])
    far_out_ref[:value] = upper[:, :tok].astype(BF)
    far_out_ref[value:] = lower[:, :tok].astype(BF)
    near_out_ref[:value] = upper[:, tok:].astype(BF)
    near_out_ref[value:] = lower[:, tok:].astype(BF)


def own_kernel(q_ref, do_ref, ds_ref, p_ref, out_ref):
    tok = q_ref.shape[2]
    value = do_ref.shape[1]
    upper, lower = partials(q_ref, do_ref, ds_ref[2 * tok :, :], p_ref[2 * tok :, :])
    out_ref[:value] = upper
    out_ref[value:] = lower


def collect_kernel(own_ref, far_ref, near_ref, out_ref):
    part = out_ref.shape[1]
    for x in range(X):
        rows = slice(x * part, (x + 1) * part)
        total = own_ref[rows] + near_ref[rows].astype(F32) + far_ref[rows].astype(F32)
        out_ref[x] = total.astype(BF)


def sum_kernel(pieces_ref, out_ref):
    total = pieces_ref[0].astype(F32)
    for x in range(1, X):
        total = total + pieces_ref[x].astype(F32)
    out_ref[...] = total.astype(BF)


def finish_kernel(mine_ref, other_ref, out_ref):
    total = (mine_ref[...].astype(F32) + other_ref[...].astype(F32)).astype(BF)
    for x in range(X):
        out_ref[x] = total


def query_kernel(far_ref, near_ref, own_ref, ds_ref, dq_ref):
    heads, _, tok = dq_ref.shape
    keys = jnp.concatenate([far_ref[...], near_ref[...], own_ref[...]], axis=1)
    for pair in range(0, heads, 2):
        out = jnp.dot(keys, ds_ref[:, pair * tok : (pair + 2) * tok], preferred_element_type=F32)
        dq_ref[pair] = out[:, :tok].astype(BF)
        dq_ref[pair + 1] = out[:, tok:].astype(BF)


def on_device(queries, latent, grad_out, lookback):
    tok, heads, width = queries.shape
    value = grad_out.shape[2]
    rows = heads * tok
    seq_size = lax.axis_size("seq")
    own = latent.T
    far = lax.ppermute(own, BOTH, shifted_pairs(seq_size, 2))
    near = lax.ppermute(own, BOTH, shifted_pairs(seq_size, 1))
    part = width // X
    turned_queries = queries.transpose(1, 2, 0)
    turned_grads = grad_out.transpose(1, 2, 0)
    params = pltpu.CompilerParams(vmem_limit_bytes=32 * 2**20)
    scores, grad_weights = pl.pallas_call(
        score_kernel,
        out_shape=(jax.ShapeDtypeStruct((tok, rows), F32),) * 2,
        in_specs=[VMEM] * 3,
        out_specs=(VMEM, VMEM),
        scratch_shapes=[pltpu.VMEM((tok, width), BF)],
        compiler_params=params,
        cost_estimate=pl.CostEstimate(
            flops=2 * rows * tok * (width + value),
            bytes_accessed=2 * rows * (width + value + 4 * tok),
            transcendentals=0,
        ),
        name="scores",
    )(turned_queries, turned_grads, own)
    near, far, scores, grad_weights = lax.optimization_barrier((near, far, scores, grad_weights))
    part_far, part_near, weights_half, grad_scores = pl.pallas_call(
        grad_kernel,
        out_shape=(
            jax.ShapeDtypeStruct((width, tok), BF),
            jax.ShapeDtypeStruct((width, tok), BF),
            jax.ShapeDtypeStruct((3 * tok, rows), BF),
            jax.ShapeDtypeStruct((3 * tok, rows), BF),
        ),
        in_specs=[VMEM] * 7,
        out_specs=(VMEM,) * 4,
        scratch_shapes=[pltpu.VMEM((2 * tok, width), BF), pltpu.VMEM((3 * tok, tok), F32)],
        compiler_params=params,
        cost_estimate=pl.CostEstimate(
            flops=2 * rows * tok * 4 * (width + value),
            bytes_accessed=2 * rows * (width + value + 10 * tok),
            transcendentals=rows * 3 * tok,
        ),
        name="grads",
    )(turned_queries, turned_grads, far, near, scores, grad_weights, lookback[None, :])

    to_far = lax.ppermute(part_far, BOTH, shifted_pairs(seq_size, -2))
    to_near = lax.ppermute(part_near, BOTH, shifted_pairs(seq_size, -1))
    part_own = pl.pallas_call(
        own_kernel,
        out_shape=jax.ShapeDtypeStruct((width, tok), F32),
        in_specs=[VMEM] * 4,
        out_specs=VMEM,
        compiler_params=params,
        cost_estimate=pl.CostEstimate(
            flops=2 * rows * tok * (width + value),
            bytes_accessed=2 * rows * (width + value + 2 * tok),
            transcendentals=0,
        ),
        name="own",
    )(turned_queries, turned_grads, grad_scores, weights_half)
    quarters = pl.pallas_call(
        collect_kernel,
        out_shape=jax.ShapeDtypeStruct((X, part, tok), BF),
        in_specs=[VMEM] * 3,
        out_specs=VMEM,
        compiler_params=params,
        name="collect",
    )(part_own, to_far, to_near)
    along_x = [[z_hi * X + x for x in range(X)] for z_hi in range(Z_HI)]
    pieces = lax.all_to_all(quarters, "head", 0, 0, axis_index_groups=along_x)
    quarter_sum = pl.pallas_call(
        sum_kernel,
        out_shape=jax.ShapeDtypeStruct((part, tok), BF),
        in_specs=[VMEM],
        out_specs=VMEM,
        compiler_params=params,
        name="sum",
    )(pieces)
    across = [(h, (h + X) % (Z_HI * X)) for h in range(Z_HI * X)]
    other_half = lax.ppermute(quarter_sum, "head", across)
    grad_queries = pl.pallas_call(
        query_kernel,
        out_shape=jax.ShapeDtypeStruct((heads, width, tok), BF),
        in_specs=[VMEM] * 4,
        out_specs=VMEM,
        compiler_params=params,
        cost_estimate=pl.CostEstimate(
            flops=2 * rows * 3 * tok * width, bytes_accessed=2 * rows * (width + 3 * tok), transcendentals=0
        ),
        name="dquery",
    )(far, near, own, grad_scores)
    other_half, grad_queries = lax.optimization_barrier((other_half, grad_queries))
    copies = pl.pallas_call(
        finish_kernel,
        out_shape=jax.ShapeDtypeStruct((X, part, tok), BF),
        in_specs=[VMEM] * 2,
        out_specs=VMEM,
        compiler_params=params,
        name="finish",
    )(quarter_sum, other_half)
    grad_latent = lax.all_to_all(copies, "head", 0, 0, axis_index_groups=along_x)
    return (grad_queries.transpose(2, 0, 1), grad_latent.reshape(width, tok).T)


def solution(mesh):
    return jax.shard_map(
        on_device,
        mesh=mesh,
        in_specs=(P("seq", "head", None), P("seq", None), P("seq", "head", None), P("seq")),
        out_specs=(P("seq", "head", None), P("seq", None)),
        check_vma=False,
    )
```
